256 devices in a mesh: section: 64 (over z, x, core), blk: 4 (over y).
Axes of the slice: x: 4, y: 4, z: 8, core: 2. Of those that a mesh axis runs over, the one named last changes fastest.
Arguments:
- held_outputs: bfloat16 [64, 128, 12288], P('section', None, 'blk'), may hold values from -6 to 6
- held_cotangents: bfloat16 [64, 128, 12288], P('section', None, 'blk'), may hold values from -6 to 6
- new_rows: bfloat16 [2, 128, 12288], P(None, 'section', 'blk'), may hold values from -6 to 6
- targets: bfloat16 [2, 128, 12288], P(None, 'section', 'blk'), may hold values from -6 to 6
- saved_first: bfloat16 [64, 2, 128, 32, 384], P('section', None, None, None, 'blk'), may hold values from -6 to 6
- up_first: bfloat16 [64, 32, 384, 384], P('section', 'blk'), may hold values from -0.3125 to 0.3125
- up_second: bfloat16 [64, 384, 32, 128], P('section', 'blk'), may hold values from -1 to 1
- down_first: bfloat16 [64, 384, 32, 128], P('section', 'blk'), may hold values from -0.5 to 0.5
- down_second: bfloat16 [64, 32, 384, 384], P('section', 'blk'), may hold values from -0.3125 to 0.3125
Outputs:
- next_outputs: bfloat16 [64, 128, 12288], P('section', None, 'blk')
- next_cotangents: bfloat16 [64, 128, 12288], P('section', None, 'blk')
- grad_up_second: bfloat16 [64, 384, 32, 128], P('section', 'blk')
- grad_down_first: bfloat16 [64, 384, 32, 128], P('section', 'blk')
The draws below stay inside these ranges and needn't reach their ends.
All inputs are finite; a program needn't handle non-finite values.
Results may differ from the reference program's by a relative error of at most 0.014.
Values may be sent and summed in bfloat16 or wider, within the bound.
A program may use at most 192 MiB of HBM per device.

```python
import jax
import jax.numpy as jnp
from jax import lax

D = 12288
BLOCK = 384
MB_ROWS = 128
TICKS = 2
NBLK = 32
HB = 128
SECTIONS = 64


def levels(rng, extent, split, smallest, high):
    loudness = 1.0
    for dim, shards_of in split:
        draws = jax.random.uniform(jax.random.fold_in(jax.random.fold_in(rng, 6), dim), (shards_of,), jnp.float32, smallest / len(split), high / len(split))
        loudness = loudness * jnp.repeat(jnp.exp(draws), extent[dim] // shards_of).reshape((-1,) + (1,) * (len(extent) - 1 - dim))
    return loudness


def noise(stream_key, extent, spread, limit, pieces=(), held_as=jnp.bfloat16):
    array = spread * jax.random.normal(stream_key, extent, jnp.float32)
    if pieces:
        array = array * levels(stream_key, extent, pieces, -0.22, 0.18)
    return jnp.clip(array, -limit, limit).astype(held_as)


def setup_inputs(seed: int = 0) -> dict:
    key_list = jax.random.split(jax.random.key(seed), 10)
    return {
        "held_outputs": noise(key_list[0], (SECTIONS, MB_ROWS, D), 1.0, 6.0, ((0, 64), (2, 4))),
        "held_cotangents": noise(key_list[1], (SECTIONS, MB_ROWS, D), 1.0, 6.0, ((0, 64), (2, 4))),
        "new_rows": noise(key_list[2], (TICKS, MB_ROWS, D), 1.0, 6.0, ((1, 64), (2, 4))),
        "targets": noise(key_list[3], (TICKS, MB_ROWS, D), 1.0, 6.0, ((1, 64), (2, 4))),
        "saved_first": noise(key_list[4], (SECTIONS, TICKS, MB_ROWS, NBLK, BLOCK), 1.0, 6.0, ((0, 64), (4, 4))),
        "up_first": noise(key_list[5], (SECTIONS, NBLK, BLOCK, BLOCK), BLOCK ** -0.5, 0.3125, ((0, 64), (1, 4))),
        "up_second": noise(key_list[6], (SECTIONS, BLOCK, NBLK, HB), NBLK ** -0.5, 1.0, ((0, 64), (1, 4))),
        "down_first": noise(key_list[7], (SECTIONS, BLOCK, NBLK, HB), HB ** -0.5, 0.5, ((0, 64), (1, 4))),
        "down_second": noise(key_list[8], (SECTIONS, NBLK, BLOCK, BLOCK), BLOCK ** -0.5, 0.3125, ((0, 64), (1, 4))),
    }


def gelu_tanh(value):
    return jax.nn.gelu(value, approximate=True)

def layer_forward(inputs, up_one, up_two, down_one, down_two):
    count = inputs.shape[0]
    blocks = inputs.reshape(count, NBLK, BLOCK).astype(jnp.float32)
    first = jnp.einsum('rji,jio->rjo', blocks, up_one.astype(jnp.float32)).astype(jnp.bfloat16)
    pre = jnp.einsum('rji,ijk->rik', first.astype(jnp.float32), up_two.astype(jnp.float32))
    act = gelu_tanh(pre).astype(jnp.bfloat16)
    mixed = jnp.einsum('rik,ijk->rji', act.astype(jnp.float32), down_one.astype(jnp.float32)).astype(jnp.bfloat16)
    branch = jnp.einsum('rji,jio->rjo', mixed.astype(jnp.float32), down_two.astype(jnp.float32))
    layer_out = (inputs.astype(jnp.float32) + branch.reshape(count, D)).astype(jnp.bfloat16)
    return (layer_out, first)

def layer_backward(incoming, kept, up_one, up_two, down_one, down_two):
    count = incoming.shape[0]
    pre = jnp.einsum('rji,ijk->rik', kept.astype(jnp.float32), up_two.astype(jnp.float32))
    act = gelu_tanh(pre).astype(jnp.bfloat16)
    grads = incoming.reshape(count, NBLK, BLOCK).astype(jnp.float32)
    back_mixed = jnp.einsum('rjo,jio->rji', grads, down_two.astype(jnp.float32)).astype(jnp.bfloat16)
    grad_down = jnp.einsum('rik,rji->ijk', act.astype(jnp.float32), back_mixed.astype(jnp.float32))
    back_act = jnp.einsum('rji,ijk->rik', back_mixed.astype(jnp.float32), down_one.astype(jnp.float32))
    unused, pull = jax.vjp(gelu_tanh, pre)
    back_pre = pull(back_act)[0].astype(jnp.bfloat16)
    grad_up = jnp.einsum('rji,rik->ijk', kept.astype(jnp.float32), back_pre.astype(jnp.float32))
    back_first = jnp.einsum('rik,ijk->rji', back_pre.astype(jnp.float32), up_two.astype(jnp.float32)).astype(jnp.bfloat16)
    back_in = jnp.einsum('rjo,jio->rji', back_first.astype(jnp.float32), up_one.astype(jnp.float32))
    result = (incoming.astype(jnp.float32) + back_in.reshape(count, D)).astype(jnp.bfloat16)
    return (result, grad_up, grad_down)

def forward_item(item):
    return layer_forward(item[0], item[1], item[2], item[3], item[4])

def backward_item(item):
    return layer_backward(item[0], item[1], item[2], item[3], item[4], item[5])

def reference(held_outputs, held_cotangents, new_rows, targets, saved_first, up_first, up_second, down_first, down_second):
    weights = (up_first, up_second, down_first, down_second)
    outputs = held_outputs
    cotangents = held_cotangents
    grad_up_sum = jnp.zeros((SECTIONS, BLOCK, NBLK, HB), jnp.float32)
    grad_down_sum = jnp.zeros((SECTIONS, BLOCK, NBLK, HB), jnp.float32)
    for tick in range(TICKS):
        inputs = jnp.concatenate([new_rows[tick][None], outputs[:-1]], axis=0)
        outputs, firsts = lax.map(forward_item, (inputs,) + weights)
        loss_grad = (outputs[-1].astype(jnp.float32) - targets[tick].astype(jnp.float32)).astype(jnp.bfloat16)
        incoming = jnp.concatenate([cotangents[1:], loss_grad[None]], axis=0)
        kept = jnp.concatenate([saved_first[:-1, tick], firsts[-1:]], axis=0)
        cotangents, grad_up, grad_down = lax.map(backward_item, (incoming, kept) + weights)
        grad_up_sum = grad_up_sum + grad_up
        grad_down_sum = grad_down_sum + grad_down
    return (outputs, cotangents, grad_up_sum.astype(jnp.bfloat16), grad_down_sum.astype(jnp.bfloat16))
```

```python
import functools

import jax
import jax.numpy as jnp
from jax import lax
from jax.experimental import pallas as pl
from jax.experimental.pallas import tpu as pltpu
from jax.sharding import PartitionSpec as P

BF = jnp.bfloat16
F32 = jnp.float32
MESH = pl.DeviceIdType.MESH
LANES = 128
TILE = 16
ROOT = 0.7978845608028654
CUBE = 0.044715


def contract(left, right, left_dim, right_dim):
    return lax.dot_general(
        left, right, (((left_dim,), (right_dim,)), ((), ())), preferred_element_type=F32
    )


def gelu_parts(value):
    square = value * value
    bent = jnp.tanh(ROOT * (value + CUBE * (square * value)))
    half = 0.5 * (1.0 + bent)
    return square, bent, half


def kernel(
    sections,
    parts,
    held_out,
    held_cot,
    rows_in,
    goals_in,
    saved_in,
    up_big_in,
    up_small_in,
    down_small_in,
    down_big_in,
    out_ref,
    cot_ref,
    grad_up_ref,
    grad_down_ref,
    up_big,
    down_big,
    up_small,
    down_small,
    up_turned,
    down_turned,
    kept,
    x_in,
    g_in,
    made_out,
    made_cot,
    sent,
    got,
    regrouped,
    staged,
    sum_up,
    sum_down,
    gathered,
    goals,
    swap,
    spread,
    load_sem,
    keep_sem,
    own_sem,
    gather_send,
    gather_recv,
    x_send,
    x_recv,
    g_send,
    g_recv,
    a_send,
    a_recv,
    store_sem,
):
    ticks, count, features = x_in.shape
    local_blocks, width = up_big.shape[0], up_big.shape[1]
    slab, all_blocks = up_small.shape[0], up_small.shape[1]
    groups = slab // TILE
    halves = all_blocks // TILE
    sec = lax.axis_index("section")
    blk = lax.axis_index("blk")
    last = sections - 1
    is_first = sec == 0
    is_last = sec == last

    barrier = pltpu.get_barrier_semaphore()

    def greet(s, b):
        pl.semaphore_signal(barrier, inc=1, device_id=(s, b), device_id_type=MESH)

    for k in range(1, parts):
        greet(sec, lax.rem(blk + k, parts))

    @pl.when(sec > 0)
    def _():
        greet(sec - 1, blk)

    @pl.when(sec < last)
    def _():
        greet(sec + 1, blk)

    for ends in (0, last):

        @pl.when(sec == ends)
        def _():
            def one(s, carry):
                @pl.when(s != ends)
                def _():
                    greet(s, blk)

                return carry

            lax.fori_loop(0, sections, one, 0)

    loads = [
        pltpu.make_async_copy(up_big_in, up_big, load_sem.at[0]),
        pltpu.make_async_copy(up_small_in, up_small, load_sem.at[1]),
        pltpu.make_async_copy(down_small_in, down_small, load_sem.at[2]),
        pltpu.make_async_copy(down_big_in, down_big, load_sem.at[3]),
    ]
    for load in loads:
        load.start()
    keeps = [
        pltpu.make_async_copy(saved_in.at[t], kept.at[t], keep_sem.at[t]) for t in range(ticks)
    ]
    for keep in keeps:
        keep.start()

    awaited = (parts - 1) + jnp.where(is_first, 0, 2) + jnp.where(is_last, 0, 2)
    pl.semaphore_wait(barrier, awaited)

    def to_end(t, which, end):
        piece = (rows_in, goals_in)[which]
        return pltpu.make_async_remote_copy(
            piece.at[t],
            gathered.at[t, sec],
            gather_send.at[t, which],
            gather_recv.at[t],
            device_id=(end, blk),
            device_id_type=MESH,
        )

    def at_end(t, which):
        piece = (rows_in, goals_in)[which]
        return pltpu.make_async_copy(piece.at[t], gathered.at[t, sec], own_sem.at[t])

    def shift(t, j, source, forward):
        column = pl.ds(pl.multiple_of(j * width, LANES), width)
        if forward:
            return pltpu.make_async_remote_copy(
                source.at[:, column],
                x_in.at[t, :, column],
                x_send.at[t],
                x_recv.at[t, j],
                device_id=(sec + 1, blk),
                device_id_type=MESH,
            )
        return pltpu.make_async_remote_copy(
            source.at[:, column],
            g_in.at[t, :, column],
            g_send.at[t],
            g_recv.at[t, j],
            device_id=(sec - 1, blk),
            device_id_type=MESH,
        )

    def send_ends(t):
        for which, end in ((0, 0), (1, last)):

            @pl.when(sec != end)
            def _():
                to_end(t, which, end).start()

            @pl.when(sec == end)
            def _():
                at_end(t, which).start()

    send_ends(0)

    def first_shift(j, carry):
        @pl.when(sec < last)
        def _():
            shift(0, j, held_out, True).start()

        return carry

    lax.fori_loop(0, local_blocks, first_shift, 0)

    def first_return(j, carry):
        @pl.when(sec > 0)
        def _():
            shift(0, j, held_cot, False).start()

        return carry

    lax.fori_loop(0, local_blocks, first_return, 0)
    for t in range(1, ticks):
        send_ends(t)

    side = TILE * TILE
    row = lax.broadcasted_iota(jnp.int32, (side, side), 0)
    col = lax.broadcasted_iota(jnp.int32, (side, side), 1)
    swap[...] = jnp.where(
        col == lax.rem(row, TILE) * TILE + lax.div(row, TILE), 1.0, 0.0
    ).astype(BF)
    per = count // sections
    tiles = TILE // per
    r_row = lax.rem(row, per)
    r_sec = lax.rem(lax.div(row, per), TILE)
    r_tile = lax.div(row, per * TILE)
    spread[...] = jnp.where(
        col == r_sec * TILE + r_tile * per + r_row, 1.0, 0.0
    ).astype(BF)

    def unpack(t, target):
        pltpu.make_async_remote_copy(
            gathered.at[t, pl.ds(0, sections - 1)],
            gathered.at[t, pl.ds(0, sections - 1)],
            gather_send.at[t, 0],
            gather_recv.at[t],
            device_id=(0, blk),
            device_id_type=MESH,
        ).wait_recv()
        pltpu.make_async_copy(rows_in.at[t], gathered.at[t, 0], own_sem.at[t]).wait()
        for a in range(sections // TILE):
            for b in range(features // LANES // tiles):
                chunk = gathered[
                    t, a * TILE : (a + 1) * TILE, b * TILE : (b + 1) * TILE, :
                ].reshape(side, LANES)
                moved = contract(spread[...], chunk, 1, 0).astype(BF)
                height = TILE * per
                for c in range(tiles):
                    lane = (b * tiles + c) * LANES
                    target[
                        t, a * height : (a + 1) * height, lane : lane + LANES
                    ] = moved[c * height : (c + 1) * height]

    for load in loads:
        load.wait()

    def turn(i, carry):
        up_turned[i] = up_small[i].T
        down_turned[i] = down_small[i].T
        return carry

    lax.fori_loop(0, slab, turn, 0, unroll=4)

    def peer(k):
        return lax.rem(blk + k, parts)

    def send_block(a, j):
        for k in (1, 3, 2):
            to = peer(k)
            pltpu.make_async_remote_copy(
                sent.at[a, to * local_blocks + j],
                got.at[a, blk * local_blocks + j],
                a_send.at[a, k],
                a_recv.at[a, k],
                device_id=(sec, to),
                device_id_type=MESH,
            ).start()

    def send_units(a, g):
        units = pl.ds(g * TILE, TILE)
        for k in (1, 3, 2):
            to = peer(k)
            pltpu.make_async_remote_copy(
                sent.at[a, pl.ds(to * local_blocks, local_blocks), units],
                got.at[a, pl.ds(blk * local_blocks, local_blocks), units],
                a_send.at[a, k],
                a_recv.at[a, k],
                device_id=(sec, to),
                device_id_type=MESH,
            ).start()

    def whole(a, k):
        to = peer(k)
        return pltpu.make_async_remote_copy(
            sent.at[a, pl.ds(to * local_blocks, local_blocks)],
            got.at[a, pl.ds(blk * local_blocks, local_blocks)],
            a_send.at[a, k],
            a_recv.at[a, k],
            device_id=(sec, to),
            device_id_type=MESH,
        )

    def arrive(a):
        for k in range(1, parts):
            whole(a, k).wait_recv()

    def put_block(a, j, value):
        for d in range(parts):
            sent[a, d * local_blocks + j] = value[d * slab : (d + 1) * slab]
        got[a, blk * local_blocks + j] = sent[a, blk * local_blocks + j]
        send_block(a, j)

    def block_of(a, j):
        return jnp.concatenate(
            [got[a, d * local_blocks + j] for d in range(parts)], axis=0
        )

    def units_in(a, g, also=None):
        units = pl.ds(g * TILE, TILE)
        for h in range(halves):
            chunk = got[a, h * TILE : (h + 1) * TILE, units, :].reshape(side, LANES)
            moved = contract(swap[...], chunk, 1, 0).astype(BF).reshape(TILE, TILE, LANES)
            regrouped[:, h * TILE : (h + 1) * TILE, :] = moved
            if also is not None:

                @pl.when(is_last)
                def _():
                    kept[also, units, h * TILE : (h + 1) * TILE, :] = moved

    def units_out(a, g):
        units = pl.ds(g * TILE, TILE)
        for h in range(halves):
            chunk = staged[:, h * TILE : (h + 1) * TILE, :].reshape(side, LANES)
            moved = contract(swap[...], chunk, 1, 0).astype(BF).reshape(TILE, TILE, LANES)
            sent[a, h * TILE : (h + 1) * TILE, units, :] = moved
        mine = pl.ds(blk * local_blocks, local_blocks)
        got[a, mine, units, :] = sent[a, mine, units, :]
        send_units(a, g)

    def forward_blocks(t, a):
        @pl.when(is_first)
        def _():
            unpack(t, x_in)

        def one(j, carry):
            @pl.when(sec > 0)
            def _():
                shift(t, j, held_out, True).wait_recv()

            column = pl.ds(pl.multiple_of(j * width, LANES), width)
            first = contract(x_in[t, :, column], up_big[j], 1, 0).astype(BF)
            put_block(a, j, first.T)
            return carry

        lax.fori_loop(0, local_blocks, one, 0)

    def forward_units(t, a, b):
        arrive(a)
        keeps[t].wait()

        def one(g, carry):
            units_in(a, g, t)
            for u in range(TILE):
                i = g * TILE + u
                pre = contract(up_turned[i], regrouped[u], 1, 0)
                square, bent, half = gelu_parts(pre)
                act = (pre * half).astype(BF)
                staged[u] = contract(down_small[i], act, 1, 0).astype(BF)
            units_out(b, g)
            return carry

        lax.fori_loop(0, groups, one, 0)

    def forward_out(t, b):
        arrive(b)

        @pl.when(is_last)
        def _():
            unpack(t, goals)

        def one(j, carry):
            column = pl.ds(pl.multiple_of(j * width, LANES), width)
            branch = contract(block_of(b, j), down_big[j], 0, 0)
            made = (x_in[t, :, column].astype(F32) + branch).astype(BF)
            made_out[t, :, column] = made
            if t + 1 < ticks:

                @pl.when(sec < last)
                def _():
                    shift(t + 1, j, made_out.at[t], True).start()

            @pl.when(is_last)
            def _():
                g_in[t, :, column] = (
                    made.astype(F32) - goals[t, :, column].astype(F32)
                ).astype(BF)

            return carry

        lax.fori_loop(0, local_blocks, one, 0)

    def backward_blocks(t, a):
        def one(j, carry):
            @pl.when(sec < last)
            def _():
                shift(t, j, held_cot, False).wait_recv()

            column = pl.ds(pl.multiple_of(j * width, LANES), width)
            back = contract(down_big[j], g_in[t, :, column], 1, 1).astype(BF)
            put_block(a, j, back)
            return carry

        lax.fori_loop(0, local_blocks, one, 0)

    def backward_units(t, a, b):
        arrive(a)

        def one(g, carry):
            units_in(a, g)
            for u in range(TILE):
                i = g * TILE + u
                held = kept[t, i]
                mixed = regrouped[u]
                pre = contract(up_turned[i], held, 1, 0)
                back_act = contract(down_turned[i], mixed, 1, 0)
                square, bent, half = gelu_parts(pre)
                act = (pre * half).astype(BF)
                slope = half + (0.5 * ROOT) * pre * (1.0 - bent * bent) * (
                    1.0 + (3.0 * CUBE) * square
                )
                back_pre = (back_act * slope).astype(BF)
                staged[u] = contract(up_small[i], back_pre, 1, 0).astype(BF)
                grad_up = contract(held, back_pre, 1, 1)
                grad_down = contract(mixed, act, 1, 1)
                if t == 0:
                    sum_up[i] = grad_up
                    sum_down[i] = grad_down
                elif t + 1 < ticks:
                    sum_up[i] += grad_up
                    sum_down[i] += grad_down
                else:
                    up_turned_out = (sum_up[i] + grad_up).astype(BF)
                    down_turned_out = (sum_down[i] + grad_down).astype(BF)
                    kept[0, i] = up_turned_out
                    kept[t, i] = down_turned_out
            units_out(b, g)
            return carry

        lax.fori_loop(0, groups, one, 0)

    def backward_out(t, b):
        arrive(b)

        def one(j, carry):
            column = pl.ds(pl.multiple_of(j * width, LANES), width)
            back_in = contract(block_of(b, j), up_big[j], 0, 1)
            made_cot[t, :, column] = (
                g_in[t, :, column].astype(F32) + back_in
            ).astype(BF)
            if t + 1 < ticks:

                @pl.when(sec > 0)
                def _():
                    shift(t + 1, j, made_cot.at[t], False).start()

            return carry

        lax.fori_loop(0, local_blocks, one, 0)

    end = ticks - 1
    forward_blocks(0, 0)
    forward_units(0, 0, 1)
    forward_out(0, 1)
    for t in range(ticks):
        backward_blocks(t, 4 * t + 2)
        if t < end:
            forward_blocks(t + 1, 4 * t + 4)
        backward_units(t, 4 * t + 2, 4 * t + 3)
        if t == end:
            stores = [
                pltpu.make_async_copy(kept.at[0], grad_up_ref, store_sem.at[1]),
                pltpu.make_async_copy(kept.at[end], grad_down_ref, store_sem.at[2]),
            ]
            for store in stores:
                store.start()
        if t < end:
            forward_units(t + 1, 4 * t + 4, 4 * t + 5)
        backward_out(t, 4 * t + 3)
        if t < end:
            forward_out(t + 1, 4 * t + 5)
            if t + 1 == end:
                stored_out = pltpu.make_async_copy(made_out.at[end], out_ref, store_sem.at[0])
                stored_out.start()
    stored_cot = pltpu.make_async_copy(made_cot.at[end], cot_ref, store_sem.at[3])
    stored_cot.start()

    for t in range(ticks):
        for which, far in ((0, 0), (1, last)):

            @pl.when(sec != far)
            def _():
                to_end(t, which, far).wait_send()

        @pl.when(sec < last)
        def _():
            pltpu.make_async_remote_copy(
                made_out.at[0],
                x_in.at[t],
                x_send.at[t],
                x_recv.at[t, 0],
                device_id=(sec + 1, blk),
                device_id_type=MESH,
            ).wait_send()

        @pl.when(sec > 0)
        def _():
            pltpu.make_async_remote_copy(
                made_cot.at[0],
                g_in.at[t],
                g_send.at[t],
                g_recv.at[t, 0],
                device_id=(sec - 1, blk),
                device_id_type=MESH,
            ).wait_send()

    for a in range(4 * ticks):
        for k in range(1, parts):
            whole(a, k).wait_send()
    for store in stores:
        store.wait()
    stored_out.wait()
    stored_cot.wait()


def local(
    held_outputs,
    held_cotangents,
    new_rows,
    targets,
    saved_first,
    up_first,
    up_second,
    down_first,
    down_second,
):
    sections = lax.axis_size("section")
    parts = lax.axis_size("blk")
    count, features = held_outputs.shape[1:]
    ticks, per = new_rows.shape[:2]
    local_blocks, width = up_first.shape[1:3]
    slab, all_blocks, hidden = up_second.shape[1:]
    exchanges = 4 * ticks

    def piece(rows):
        tiles = rows.reshape(ticks, per, features // LANES, LANES)
        return tiles.transpose(0, 2, 1, 3).reshape(ticks, per * features // LANES, LANES)

    saved = saved_first[0].transpose(0, 3, 2, 1)
    anywhere = pl.BlockSpec(memory_space=pl.ANY)
    vmem = pltpu.VMEM
    dma = pltpu.SemaphoreType.DMA
    outs = pl.pallas_call(
        functools.partial(kernel, sections, parts),
        out_shape=(
            jax.ShapeDtypeStruct((count, features), BF),
            jax.ShapeDtypeStruct((count, features), BF),
            jax.ShapeDtypeStruct((slab, all_blocks, hidden), BF),
            jax.ShapeDtypeStruct((slab, all_blocks, hidden), BF),
        ),
        in_specs=[anywhere] * 9,
        out_specs=(anywhere,) * 4,
        scratch_shapes=[
            vmem((local_blocks, width, width), BF),
            vmem((local_blocks, width, width), BF),
            vmem((slab, all_blocks, hidden), BF),
            vmem((slab, all_blocks, hidden), BF),
            vmem((slab, hidden, all_blocks), BF),
            vmem((slab, hidden, all_blocks), BF),
            vmem((ticks, slab, all_blocks, count), BF),
            vmem((ticks, count, features), BF),
            vmem((ticks, count, features), BF),
            vmem((ticks, count, features), BF),
            vmem((ticks, count, features), BF),
            vmem((exchanges, all_blocks, slab, count), BF),
            vmem((exchanges, all_blocks, slab, count), BF),
            vmem((TILE, all_blocks, count), BF),
            vmem((TILE, all_blocks, count), BF),
            vmem((slab, all_blocks, hidden), F32),
            vmem((slab, all_blocks, hidden), F32),
            vmem((ticks, sections, per * features // LANES, LANES), BF),
            vmem((ticks, count, features), BF),
            vmem((TILE * TILE, TILE * TILE), BF),
            vmem((TILE * TILE, TILE * TILE), BF),
            dma((4,)),
            dma((ticks,)),
            dma((ticks,)),
            dma((ticks, 2)),
            dma((ticks,)),
            dma((ticks,)),
            dma((ticks, local_blocks)),
            dma((ticks,)),
            dma((ticks, local_blocks)),
            dma((exchanges, parts)),
            dma((exchanges, parts)),
            dma((4,)),
        ],
        compiler_params=pltpu.CompilerParams(
            collective_id=0, has_side_effects=True, vmem_limit_bytes=60 * 1024 * 1024
        ),
        name="relay_window",
    )(
        held_outputs[0],
        held_cotangents[0],
        piece(new_rows),
        piece(targets),
        saved,
        up_first[0],
        up_second[0],
        down_first[0],
        down_second[0],
    )
    return tuple(out[None] for out in outs)


def solution(mesh):
    placed = (
        P("section", None, "blk"),
        P("section", None, "blk"),
        P(None, "section", "blk"),
        P(None, "section", "blk"),
        P("section", None, None, None, "blk"),
        P("section", "blk", None, None),
        P("section", "blk", None, None),
        P("section", "blk", None, None),
        P("section", "blk", None, None),
    )
    return jax.shard_map(
        local,
        mesh=mesh,
        in_specs=placed,
        out_specs=(
            P("section", None, "blk"),
            P("section", None, "blk"),
            P("section", "blk", None, None),
            P("section", "blk", None, None),
        ),
        check_vma=False,
    )
```

```python
import functools

import jax
import jax.numpy as jnp
from jax import lax
from jax.experimental import pallas as pl
from jax.experimental.pallas import tpu as pltpu
from jax.sharding import PartitionSpec as P

BF = jnp.bfloat16
F32 = jnp.float32
MESH = pl.DeviceIdType.MESH
LANES = 128
TILE = 16
ROOT = 0.7978845608028654
CUBE = 0.044715


def contract(left, right, left_dim, right_dim):
    return lax.dot_general(
        left, right, (((left_dim,), (right_dim,)), ((), ())), preferred_element_type=F32
    )


def gelu_parts(value):
    square = value * value
    bent = jnp.tanh(ROOT * (value + CUBE * (square * value)))
    half = 0.5 * (1.0 + bent)
    return square, bent, half


def kernel(
    sections,
    parts,
    held_out,
    held_cot,
    rows_in,
    goals_in,
    saved_in,
    up_big_in,
    up_small_in,
    down_small_in,
    down_big_in,
    out_ref,
    cot_ref,
    grad_up_ref,
    grad_down_ref,
    up_big,
    down_big,
    up_small,
    down_small,
    up_turned,
    down_turned,
    kept,
    x_in,
    g_in,
    made_out,
    made_cot,
    sent,
    got,
    regrouped,
    staged,
    sum_up,
    sum_down,
    gathered,
    goals,
    swap,
    spread,
    load_sem,
    keep_sem,
    own_sem,
    gather_send,
    gather_recv,
    x_send,
    x_recv,
    g_send,
    g_recv,
    a_send,
    a_recv,
    store_sem,
):
    ticks, count, features = x_in.shape
    local_blocks, width = up_big.shape[0], up_big.shape[1]
    slab, all_blocks = up_small.shape[0], up_small.shape[1]
    groups = slab // TILE
    halves = all_blocks // TILE
    sec = lax.axis_index("section")
    blk = lax.axis_index("blk")
    last = sections - 1
    is_first = sec == 0
    is_last = sec == last
    is_even = lax.rem(sec, 2) == 0
    is_odd = jnp.logical_not(jnp.logical_or(is_even, is_last))

    barrier = pltpu.get_barrier_semaphore()

    def greet(s, b):
        pl.semaphore_signal(barrier, inc=1, device_id=(s, b), device_id_type=MESH)

    for k in range(1, parts):
        greet(sec, lax.rem(blk + k, parts))

    @pl.when(sec > 0)
    def _():
        greet(sec - 1, blk)

    @pl.when(sec < last)
    def _():
        greet(sec + 1, blk)

    for ends in (0, last):

        @pl.when(sec == ends)
        def _():
            def one(s, carry):
                @pl.when(s != ends)
                def _():
                    greet(s, blk)

                return carry

            lax.fori_loop(0, sections, one, 0)

    loads = [
        pltpu.make_async_copy(up_big_in, up_big, load_sem.at[0]),
        pltpu.make_async_copy(up_small_in, up_small, load_sem.at[1]),
        pltpu.make_async_copy(down_small_in, down_small, load_sem.at[2]),
        pltpu.make_async_copy(down_big_in, down_big, load_sem.at[3]),
    ]
    for k in (1, 2, 0, 3):
        loads[k].start()
    keeps = [
        pltpu.make_async_copy(saved_in.at[t], kept.at[t], keep_sem.at[t]) for t in range(ticks)
    ]
    for keep in keeps:
        keep.start()

    side = TILE * TILE
    row = lax.broadcasted_iota(jnp.int32, (side, side), 0)
    col = lax.broadcasted_iota(jnp.int32, (side, side), 1)
    swap[...] = jnp.where(
        col == lax.rem(row, TILE) * TILE + lax.div(row, TILE), 1.0, 0.0
    ).astype(BF)
    per = count // sections
    tiles = TILE // per
    r_row = lax.rem(row, per)
    r_sec = lax.rem(lax.div(row, per), TILE)
    r_tile = lax.div(row, per * TILE)
    spread[...] = jnp.where(
        col == r_sec * TILE + r_tile * per + r_row, 1.0, 0.0
    ).astype(BF)

    for load in loads[1:3]:
        load.wait()

    def turn(i, carry):
        up_turned[i] = up_small[i].T
        down_turned[i] = down_small[i].T
        return carry

    lax.fori_loop(0, slab, turn, 0, unroll=4)

    awaited = (parts - 1) + jnp.where(is_first, 0, 2) + jnp.where(is_last, 0, 2)
    pl.semaphore_wait(barrier, awaited)

    def to_end(t, which, end):
        piece = (rows_in, goals_in)[which]
        return pltpu.make_async_remote_copy(
            piece.at[t],
            gathered.at[t, sec],
            gather_send.at[t, which],
            gather_recv.at[t],
            device_id=(end, blk),
            device_id_type=MESH,
        )

    def at_end(t, which):
        piece = (rows_in, goals_in)[which]
        return pltpu.make_async_copy(piece.at[t], gathered.at[t, sec], own_sem.at[t])

    def shift(t, j, source, forward):
        column = pl.ds(pl.multiple_of(j * width, LANES), width)
        if forward:
            return pltpu.make_async_remote_copy(
                source.at[:, column],
                x_in.at[t, :, column],
                x_send.at[t],
                x_recv.at[t, j],
                device_id=(sec + 1, blk),
                device_id_type=MESH,
            )
        return pltpu.make_async_remote_copy(
            source.at[:, column],
            g_in.at[t, :, column],
            g_send.at[t],
            g_recv.at[t, j],
            device_id=(sec - 1, blk),
            device_id_type=MESH,
        )

    def send_ends(t):
        for which, end in ((0, 0), (1, last)):

            @pl.when(sec != end)
            def _():
                to_end(t, which, end).start()

            @pl.when(sec == end)
            def _():
                at_end(t, which).start()

    send_ends(0)

    def first_shift(j, carry):
        @pl.when(sec < last)
        def _():
            shift(0, j, held_out, True).start()

        return carry

    lax.fori_loop(0, local_blocks, first_shift, 0)

    def first_return(j, carry):
        @pl.when(sec > 0)
        def _():
            shift(0, j, held_cot, False).start()

        return carry

    lax.fori_loop(0, local_blocks, first_return, 0)
    for t in range(1, ticks):
        send_ends(t)

    def unpack(t, target):
        pltpu.make_async_remote_copy(
            gathered.at[t, pl.ds(0, sections - 1)],
            gathered.at[t, pl.ds(0, sections - 1)],
            gather_send.at[t, 0],
            gather_recv.at[t],
            device_id=(0, blk),
            device_id_type=MESH,
        ).wait_recv()
        pltpu.make_async_copy(rows_in.at[t], gathered.at[t, 0], own_sem.at[t]).wait()
        for a in range(sections // TILE):
            for b in range(features // LANES // tiles):
                chunk = gathered[
                    t, a * TILE : (a + 1) * TILE, b * TILE : (b + 1) * TILE, :
                ].reshape(side, LANES)
                moved = contract(spread[...], chunk, 1, 0).astype(BF)
                height = TILE * per
                for c in range(tiles):
                    lane = (b * tiles + c) * LANES
                    target[
                        t, a * height : (a + 1) * height, lane : lane + LANES
                    ] = moved[c * height : (c + 1) * height]

    loads[0].wait()
    loads[3].wait()
    for keep in keeps:
        keep.wait()

    def peer(k):
        return lax.rem(blk + k, parts)

    def send_block(a, j):
        for k in (1, 3, 2):
            to = peer(k)
            pltpu.make_async_remote_copy(
                sent.at[a, to * local_blocks + j],
                got.at[a, blk * local_blocks + j],
                a_send.at[a, k],
                a_recv.at[a, k],
                device_id=(sec, to),
                device_id_type=MESH,
            ).start()

    def send_units(a, g):
        units = pl.ds(g * TILE, TILE)
        for k in (1, 3, 2):
            to = peer(k)
            pltpu.make_async_remote_copy(
                sent.at[a, pl.ds(to * local_blocks, local_blocks), units],
                got.at[a, pl.ds(blk * local_blocks, local_blocks), units],
                a_send.at[a, k],
                a_recv.at[a, k],
                device_id=(sec, to),
                device_id_type=MESH,
            ).start()

    def whole(a, k):
        to = peer(k)
        return pltpu.make_async_remote_copy(
            sent.at[a, pl.ds(to * local_blocks, local_blocks)],
            got.at[a, pl.ds(blk * local_blocks, local_blocks)],
            a_send.at[a, k],
            a_recv.at[a, k],
            device_id=(sec, to),
            device_id_type=MESH,
        )

    def arrive(a):
        for k in range(1, parts):
            whole(a, k).wait_recv()

    def put_block(a, j, value):
        for d in range(parts):
            sent[a, d * local_blocks + j] = value[d * slab : (d + 1) * slab]
        got[a, blk * local_blocks + j] = sent[a, blk * local_blocks + j]
        send_block(a, j)

    def block_of(a, j):
        return jnp.concatenate(
            [got[a, d * local_blocks + j] for d in range(parts)], axis=0
        )

    def units_in(a, g):
        units = pl.ds(g * TILE, TILE)
        for h in range(halves):
            chunk = got[a, h * TILE : (h + 1) * TILE, units, :].reshape(side, LANES)
            moved = contract(swap[...], chunk, 1, 0).astype(BF).reshape(TILE, TILE, LANES)
            regrouped[:, h * TILE : (h + 1) * TILE, :] = moved

    def units_out(a, g):
        units = pl.ds(g * TILE, TILE)
        for h in range(halves):
            chunk = staged[:, h * TILE : (h + 1) * TILE, :].reshape(side, LANES)
            moved = contract(swap[...], chunk, 1, 0).astype(BF).reshape(TILE, TILE, LANES)
            sent[a, h * TILE : (h + 1) * TILE, units, :] = moved
        mine = pl.ds(blk * local_blocks, local_blocks)
        got[a, mine, units, :] = sent[a, mine, units, :]
        send_units(a, g)

    def forward_blocks(t, a):
        @pl.when(is_first)
        def _():
            unpack(t, x_in)

        def one(j, carry):
            @pl.when(sec > 0)
            def _():
                shift(t, j, held_out, True).wait_recv()

            column = pl.ds(pl.multiple_of(j * width, LANES), width)
            first = contract(x_in[t, :, column], up_big[j], 1, 0).astype(BF)
            put_block(a, j, first.T)
            return carry

        lax.fori_loop(0, local_blocks, one, 0)

    def forward_units(t, a, b):
        arrive(a)

        def one(g, carry):
            units_in(a, g)
            for u in range(TILE):
                i = g * TILE + u
                pre = contract(up_turned[i], regrouped[u], 1, 0)
                square, bent, half = gelu_parts(pre)
                act = (pre * half).astype(BF)
                staged[u] = contract(down_small[i], act, 1, 0).astype(BF)
            units_out(b, g)

            @pl.when(is_last)
            def _():
                kept[t, pl.ds(g * TILE, TILE)] = regrouped[...]

            return carry

        lax.fori_loop(0, groups, one, 0)

    def forward_out(t, b):
        arrive(b)

        @pl.when(is_last)
        def _():
            unpack(t, goals)

        def one(j, carry):
            column = pl.ds(pl.multiple_of(j * width, LANES), width)
            branch = contract(block_of(b, j), down_big[j], 0, 0)
            made = (x_in[t, :, column].astype(F32) + branch).astype(BF)
            made_out[t, :, column] = made
            if t + 1 < ticks:

                @pl.when(sec < last)
                def _():
                    shift(t + 1, j, made_out.at[t], True).start()

            @pl.when(is_last)
            def _():
                g_in[t, :, column] = (
                    made.astype(F32) - goals[t, :, column].astype(F32)
                ).astype(BF)

            return carry

        lax.fori_loop(0, local_blocks, one, 0)

    def backward_blocks(t, a):
        def one(j, carry):
            @pl.when(sec < last)
            def _():
                shift(t, j, held_cot, False).wait_recv()

            column = pl.ds(pl.multiple_of(j * width, LANES), width)
            back = contract(down_big[j], g_in[t, :, column], 1, 1).astype(BF)
            put_block(a, j, back)
            return carry

        lax.fori_loop(0, local_blocks, one, 0)

    def backward_units(t, a, b):
        arrive(a)

        def one(g, carry):
            units_in(a, g)
            for u in range(TILE):
                i = g * TILE + u
                held = kept[t, i]
                mixed = regrouped[u]
                pre = contract(up_turned[i], held, 1, 0)
                back_act = contract(down_turned[i], mixed, 1, 0)
                square, bent, half = gelu_parts(pre)
                act = (pre * half).astype(BF)
                slope = half + (0.5 * ROOT) * pre * (1.0 - bent * bent) * (
                    1.0 + (3.0 * CUBE) * square
                )
                back_pre = (back_act * slope).astype(BF)
                staged[u] = contract(up_small[i], back_pre, 1, 0).astype(BF)
                grad_up = contract(held, back_pre, 1, 1)
                grad_down = contract(mixed, act, 1, 1)
                if t == 0:
                    sum_up[i] = grad_up
                    sum_down[i] = grad_down
                elif t + 1 < ticks:
                    sum_up[i] += grad_up
                    sum_down[i] += grad_down
                else:
                    up_turned_out = (sum_up[i] + grad_up).astype(BF)
                    down_turned_out = (sum_down[i] + grad_down).astype(BF)
                    kept[0, i] = up_turned_out
                    kept[t, i] = down_turned_out
            units_out(b, g)
            return carry

        lax.fori_loop(0, groups, one, 0)

    def backward_out(t, b):
        arrive(b)

        def one(j, carry):
            column = pl.ds(pl.multiple_of(j * width, LANES), width)
            back_in = contract(block_of(b, j), up_big[j], 0, 1)
            made_cot[t, :, column] = (
                g_in[t, :, column].astype(F32) + back_in
            ).astype(BF)
            if t + 1 < ticks:

                @pl.when(sec > 0)
                def _():
                    shift(t + 1, j, made_cot.at[t], False).start()

            return carry

        lax.fori_loop(0, local_blocks, one, 0)

    end = ticks - 1
    stores = [
        pltpu.make_async_copy(made_out.at[end], out_ref, store_sem.at[0]),
        pltpu.make_async_copy(kept.at[0], grad_up_ref, store_sem.at[1]),
        pltpu.make_async_copy(kept.at[end], grad_down_ref, store_sem.at[2]),
        pltpu.make_async_copy(made_cot.at[end], cot_ref, store_sem.at[3]),
    ]

    def stage(kind, t):
        a = 4 * t
        if kind == "FB":
            forward_blocks(t, a)
        elif kind == "FU":
            forward_units(t, a, a + 1)
        elif kind == "FO":
            forward_out(t, a + 1)
            if t == end:
                stores[0].start()
        elif kind == "BB":
            backward_blocks(t, a + 2)
        elif kind == "BU":
            backward_units(t, a + 2, a + 3)
            if t == end:
                stores[1].start()
                stores[2].start()
        else:
            backward_out(t, a + 3)
            if t == end:
                stores[3].start()

    def only(who, *steps):
        @pl.when(who)
        def _():
            for kind, t in steps:
                stage(kind, t)

    for t in range(ticks):
        early, late = (is_even, is_odd) if t % 2 == 0 else (is_odd, is_even)
        only(early, ("BB", t))
        stage("FB", t)
        if t > 0:
            only(is_last, ("BO", t - 1))
        only(late, ("BB", t))
        only(early, ("BU", t))
        stage("FU", t)
        only(late, ("BU", t))
        only(early, ("BO", t))
        stage("FO", t)
        only(late, ("BO", t))
        only(is_last, ("BB", t), ("BU", t))
    only(is_last, ("BO", end))

    for t in range(ticks):
        for which, far in ((0, 0), (1, last)):

            @pl.when(sec != far)
            def _():
                to_end(t, which, far).wait_send()

        @pl.when(sec < last)
        def _():
            pltpu.make_async_remote_copy(
                made_out.at[0],
                x_in.at[t],
                x_send.at[t],
                x_recv.at[t, 0],
                device_id=(sec + 1, blk),
                device_id_type=MESH,
            ).wait_send()

        @pl.when(sec > 0)
        def _():
            pltpu.make_async_remote_copy(
                made_cot.at[0],
                g_in.at[t],
                g_send.at[t],
                g_recv.at[t, 0],
                device_id=(sec - 1, blk),
                device_id_type=MESH,
            ).wait_send()

    for a in range(4 * ticks):
        for k in range(1, parts):
            whole(a, k).wait_send()
    for store in stores:
        store.wait()


def local(
    held_outputs,
    held_cotangents,
    new_rows,
    targets,
    saved_first,
    up_first,
    up_second,
    down_first,
    down_second,
):
    sections = lax.axis_size("section")
    parts = lax.axis_size("blk")
    count, features = held_outputs.shape[1:]
    ticks, per = new_rows.shape[:2]
    local_blocks, width = up_first.shape[1:3]
    slab, all_blocks, hidden = up_second.shape[1:]
    exchanges = 4 * ticks

    def piece(rows):
        tiles = rows.reshape(ticks, per, features // LANES, LANES)
        return tiles.transpose(0, 2, 1, 3).reshape(ticks, per * features // LANES, LANES)

    saved = saved_first[0].transpose(0, 3, 2, 1)
    anywhere = pl.BlockSpec(memory_space=pl.ANY)
    vmem = pltpu.VMEM
    dma = pltpu.SemaphoreType.DMA
    outs = pl.pallas_call(
        functools.partial(kernel, sections, parts),
        out_shape=(
            jax.ShapeDtypeStruct((count, features), BF),
            jax.ShapeDtypeStruct((count, features), BF),
            jax.ShapeDtypeStruct((slab, all_blocks, hidden), BF),
            jax.ShapeDtypeStruct((slab, all_blocks, hidden), BF),
        ),
        in_specs=[anywhere] * 9,
        out_specs=(anywhere,) * 4,
        scratch_shapes=[
            vmem((local_blocks, width, width), BF),
            vmem((local_blocks, width, width), BF),
            vmem((slab, all_blocks, hidden), BF),
            vmem((slab, all_blocks, hidden), BF),
            vmem((slab, hidden, all_blocks), BF),
            vmem((slab, hidden, all_blocks), BF),
            vmem((ticks, slab, all_blocks, count), BF),
            vmem((ticks, count, features), BF),
            vmem((ticks, count, features), BF),
            vmem((ticks, count, features), BF),
            vmem((ticks, count, features), BF),
            vmem((exchanges, all_blocks, slab, count), BF),
            vmem((exchanges, all_blocks, slab, count), BF),
            vmem((TILE, all_blocks, count), BF),
            vmem((TILE, all_blocks, count), BF),
            vmem((slab, all_blocks, hidden), F32),
            vmem((slab, all_blocks, hidden), F32),
            vmem((ticks, sections, per * features // LANES, LANES), BF),
            vmem((ticks, count, features), BF),
            vmem((TILE * TILE, TILE * TILE), BF),
            vmem((TILE * TILE, TILE * TILE), BF),
            dma((4,)),
            dma((ticks,)),
            dma((ticks,)),
            dma((ticks, 2)),
            dma((ticks,)),
            dma((ticks,)),
            dma((ticks, local_blocks)),
            dma((ticks,)),
            dma((ticks, local_blocks)),
            dma((exchanges, parts)),
            dma((exchanges, parts)),
            dma((4,)),
        ],
        compiler_params=pltpu.CompilerParams(
            collective_id=0, has_side_effects=True, vmem_limit_bytes=60 * 1024 * 1024
        ),
        name="relay_window",
    )(
        held_outputs[0],
        held_cotangents[0],
        piece(new_rows),
        piece(targets),
        saved,
        up_first[0],
        up_second[0],
        down_first[0],
        down_second[0],
    )
    return tuple(out[None] for out in outs)


def solution(mesh):
    placed = (
        P("section", None, "blk"),
        P("section", None, "blk"),
        P(None, "section", "blk"),
        P(None, "section", "blk"),
        P("section", None, None, None, "blk"),
        P("section", "blk", None, None),
        P("section", "blk", None, None),
        P("section", "blk", None, None),
        P("section", "blk", None, None),
    )
    return jax.shard_map(
        local,
        mesh=mesh,
        in_specs=placed,
        out_specs=(
            P("section", None, "blk"),
            P("section", None, "blk"),
            P("section", "blk", None, None),
            P("section", "blk", None, None),
        ),
        check_vma=False,
    )
```

```python
import functools

import jax
import jax.numpy as jnp
from jax import lax
from jax.experimental import pallas as pl
from jax.experimental.pallas import tpu as pltpu
from jax.sharding import PartitionSpec as P

BF = jnp.bfloat16
F32 = jnp.float32
MESH = pl.DeviceIdType.MESH
LANES = 128
TILE = 16
ROOT = 0.7978845608028654
CUBE = 0.044715


def contract(left, right, left_dim, right_dim):
    return lax.dot_general(
        left, right, (((left_dim,), (right_dim,)), ((), ())), preferred_element_type=F32
    )


def gelu_parts(value):
    square = value * value
    bent = jnp.tanh(ROOT * (value + CUBE * (square * value)))
    half = 0.5 * (1.0 + bent)
    return square, bent, half


def kernel(
    sections,
    parts,
    held_out,
    held_cot,
    rows_in,
    goals_in,
    saved_in,
    up_big_in,
    up_small_in,
    down_small_in,
    down_big_in,
    out_ref,
    cot_ref,
    grad_up_ref,
    grad_down_ref,
    up_big,
    down_big,
    up_small,
    down_small,
    up_turned,
    down_turned,
    kept,
    x_in,
    g_in,
    made_out,
    made_cot,
    sent,
    got,
    regrouped,
    staged,
    sum_up,
    sum_down,
    gathered,
    goals,
    swap,
    spread,
    load_sem,
    keep_sem,
    own_sem,
    gather_send,
    gather_recv,
    x_send,
    x_recv,
    g_send,
    g_recv,
    a_send,
    a_recv,
    store_sem,
):
    ticks, count, features = x_in.shape
    local_blocks, width = up_big.shape[0], up_big.shape[1]
    slab, all_blocks = up_small.shape[0], up_small.shape[1]
    groups = slab // TILE
    halves = all_blocks // TILE
    sec = lax.axis_index("section")
    blk = lax.axis_index("blk")
    last = sections - 1
    is_first = sec == 0
    is_last = sec == last
    is_even = lax.rem(sec, 2) == 0
    is_odd = jnp.logical_not(jnp.logical_or(is_even, is_last))

    barrier = pltpu.get_barrier_semaphore()

    def greet(s, b):
        pl.semaphore_signal(barrier, inc=1, device_id=(s, b), device_id_type=MESH)

    for k in range(1, parts):
        greet(sec, lax.rem(blk + k, parts))

    @pl.when(sec > 0)
    def _():
        greet(sec - 1, blk)

    @pl.when(sec < last)
    def _():
        greet(sec + 1, blk)

    for ends in (0, last):

        @pl.when(sec == ends)
        def _():
            def one(s, carry):
                @pl.when(s != ends)
                def _():
                    greet(s, blk)

                return carry

            lax.fori_loop(0, sections, one, 0)

    loads = [
        pltpu.make_async_copy(up_big_in, up_big, load_sem.at[0]),
        pltpu.make_async_copy(up_small_in, up_small, load_sem.at[1]),
        pltpu.make_async_copy(down_small_in, down_small, load_sem.at[2]),
        pltpu.make_async_copy(down_big_in, down_big, load_sem.at[3]),
    ]
    for k in (1, 2, 0, 3):
        loads[k].start()
    keeps = [
        pltpu.make_async_copy(saved_in.at[t], kept.at[t], keep_sem.at[t]) for t in range(ticks)
    ]
    for keep in keeps:
        keep.start()

    side = TILE * TILE
    row = lax.broadcasted_iota(jnp.int32, (side, side), 0)
    col = lax.broadcasted_iota(jnp.int32, (side, side), 1)
    swap[...] = jnp.where(
        col == lax.rem(row, TILE) * TILE + lax.div(row, TILE), 1.0, 0.0
    ).astype(BF)
    per = count // sections
    tiles = TILE // per
    r_row = lax.rem(row, per)
    r_sec = lax.rem(lax.div(row, per), TILE)
    r_tile = lax.div(row, per * TILE)
    spread[...] = jnp.where(
        col == r_sec * TILE + r_tile * per + r_row, 1.0, 0.0
    ).astype(BF)

    for load in loads[1:3]:
        load.wait()

    def turn(i, carry):
        up_turned[i] = up_small[i].T
        down_turned[i] = down_small[i].T
        return carry

    lax.fori_loop(0, slab, turn, 0, unroll=4)

    awaited = (parts - 1) + jnp.where(is_first, 0, 2) + jnp.where(is_last, 0, 2)
    pl.semaphore_wait(barrier, awaited)

    def to_end(t, which, end):
        piece = (rows_in, goals_in)[which]
        return pltpu.make_async_remote_copy(
            piece.at[t],
            gathered.at[t, sec],
            gather_send.at[t, which],
            gather_recv.at[t],
            device_id=(end, blk),
            device_id_type=MESH,
        )

    def at_end(t, which):
        piece = (rows_in, goals_in)[which]
        return pltpu.make_async_copy(piece.at[t], gathered.at[t, sec], own_sem.at[t])

    def shift(t, j, source, forward):
        column = pl.ds(pl.multiple_of(j * width, LANES), width)
        if forward:
            return pltpu.make_async_remote_copy(
                source.at[:, column],
                x_in.at[t, :, column],
                x_send.at[t],
                x_recv.at[t, j],
                device_id=(sec + 1, blk),
                device_id_type=MESH,
            )
        return pltpu.make_async_remote_copy(
            source.at[:, column],
            g_in.at[t, :, column],
            g_send.at[t],
            g_recv.at[t, j],
            device_id=(sec - 1, blk),
            device_id_type=MESH,
        )

    def send_ends(t):
        for which, end in ((0, 0), (1, last)):

            @pl.when(sec != end)
            def _():
                to_end(t, which, end).start()

            @pl.when(sec == end)
            def _():
                at_end(t, which).start()

    send_ends(0)

    def first_shift(j, carry):
        @pl.when(sec < last)
        def _():
            shift(0, j, held_out, True).start()

        return carry

    lax.fori_loop(0, local_blocks, first_shift, 0)

    def first_return(j, carry):
        @pl.when(sec > 0)
        def _():
            shift(0, j, held_cot, False).start()

        return carry

    lax.fori_loop(0, local_blocks, first_return, 0)
    for t in range(1, ticks):
        send_ends(t)

    def unpack(t, target):
        pltpu.make_async_remote_copy(
            gathered.at[t, pl.ds(0, sections - 1)],
            gathered.at[t, pl.ds(0, sections - 1)],
            gather_send.at[t, 0],
            gather_recv.at[t],
            device_id=(0, blk),
            device_id_type=MESH,
        ).wait_recv()
        pltpu.make_async_copy(rows_in.at[t], gathered.at[t, 0], own_sem.at[t]).wait()
        for a in range(sections // TILE):
            for b in range(features // LANES // tiles):
                chunk = gathered[
                    t, a * TILE : (a + 1) * TILE, b * TILE : (b + 1) * TILE, :
                ].reshape(side, LANES)
                moved = contract(spread[...], chunk, 1, 0).astype(BF)
                height = TILE * per
                for c in range(tiles):
                    lane = (b * tiles + c) * LANES
                    target[
                        t, a * height : (a + 1) * height, lane : lane + LANES
                    ] = moved[c * height : (c + 1) * height]

    loads[0].wait()
    loads[3].wait()
    for keep in keeps:
        keep.wait()

    def peer(k):
        return lax.rem(blk + k, parts)

    def send_block(a, j):
        for k in (1, 3, 2):
            to = peer(k)
            pltpu.make_async_remote_copy(
                sent.at[a, to * local_blocks + j],
                got.at[a, blk * local_blocks + j],
                a_send.at[a, k],
                a_recv.at[a, k],
                device_id=(sec, to),
                device_id_type=MESH,
            ).start()

    def send_units(a, g):
        units = pl.ds(g * TILE, TILE)
        for k in (1, 3, 2):
            to = peer(k)
            pltpu.make_async_remote_copy(
                sent.at[a, pl.ds(to * local_blocks, local_blocks), units],
                got.at[a, pl.ds(blk * local_blocks, local_blocks), units],
                a_send.at[a, k],
                a_recv.at[a, k],
                device_id=(sec, to),
                device_id_type=MESH,
            ).start()

    def whole(a, k):
        to = peer(k)
        return pltpu.make_async_remote_copy(
            sent.at[a, pl.ds(to * local_blocks, local_blocks)],
            got.at[a, pl.ds(blk * local_blocks, local_blocks)],
            a_send.at[a, k],
            a_recv.at[a, k],
            device_id=(sec, to),
            device_id_type=MESH,
        )

    def arrive(a):
        for k in range(1, parts):
            whole(a, k).wait_recv()

    def put_block(a, j, value):
        for d in range(parts):
            sent[a, d * local_blocks + j] = value[d * slab : (d + 1) * slab]
        got[a, blk * local_blocks + j] = sent[a, blk * local_blocks + j]
        send_block(a, j)

    def block_of(a, j):
        return jnp.concatenate(
            [got[a, d * local_blocks + j] for d in range(parts)], axis=0
        )

    def units_in(a, g):
        units = pl.ds(g * TILE, TILE)
        for h in range(halves):
            chunk = got[a, h * TILE : (h + 1) * TILE, units, :].reshape(side, LANES)
            moved = contract(swap[...], chunk, 1, 0).astype(BF).reshape(TILE, TILE, LANES)
            regrouped[:, h * TILE : (h + 1) * TILE, :] = moved

    def units_out(a, g):
        units = pl.ds(g * TILE, TILE)
        for h in range(halves):
            chunk = staged[:, h * TILE : (h + 1) * TILE, :].reshape(side, LANES)
            moved = contract(swap[...], chunk, 1, 0).astype(BF).reshape(TILE, TILE, LANES)
            sent[a, h * TILE : (h + 1) * TILE, units, :] = moved
        mine = pl.ds(blk * local_blocks, local_blocks)
        got[a, mine, units, :] = sent[a, mine, units, :]
        send_units(a, g)

    def forward_blocks(t, a):
        @pl.when(is_first)
        def _():
            unpack(t, x_in)

        def one(j, carry):
            @pl.when(sec > 0)
            def _():
                shift(t, j, held_out, True).wait_recv()

            column = pl.ds(pl.multiple_of(j * width, LANES), width)
            first = contract(x_in[t, :, column], up_big[j], 1, 0).astype(BF)
            put_block(a, j, first.T)
            return carry

        lax.fori_loop(0, local_blocks, one, 0)

    def forward_units(t, a, b):
        arrive(a)

        def one(g, carry):
            units_in(a, g)

            def unit(u, carry):
                i = g * TILE + u
                pre = contract(up_turned[i], regrouped[u], 1, 0)
                square, bent, half = gelu_parts(pre)
                act = (pre * half).astype(BF)
                staged[u] = contract(down_small[i], act, 1, 0).astype(BF)
                return carry

            lax.fori_loop(0, TILE, unit, 0, unroll=4)
            units_out(b, g)

            @pl.when(is_last)
            def _():
                kept[t, pl.ds(g * TILE, TILE)] = regrouped[...]

            return carry

        lax.fori_loop(0, groups, one, 0)

    def forward_out(t, b):
        arrive(b)

        @pl.when(is_last)
        def _():
            unpack(t, goals)

        def one(j, carry):
            column = pl.ds(pl.multiple_of(j * width, LANES), width)
            branch = contract(block_of(b, j), down_big[j], 0, 0)
            made = (x_in[t, :, column].astype(F32) + branch).astype(BF)
            made_out[t, :, column] = made
            if t + 1 < ticks:

                @pl.when(sec < last)
                def _():
                    shift(t + 1, j, made_out.at[t], True).start()

            @pl.when(is_last)
            def _():
                g_in[t, :, column] = (
                    made.astype(F32) - goals[t, :, column].astype(F32)
                ).astype(BF)

            return carry

        lax.fori_loop(0, local_blocks, one, 0)

    def backward_blocks(t, a):
        def one(j, carry):
            @pl.when(sec < last)
            def _():
                shift(t, j, held_cot, False).wait_recv()

            column = pl.ds(pl.multiple_of(j * width, LANES), width)
            back = contract(down_big[j], g_in[t, :, column], 1, 1).astype(BF)
            put_block(a, j, back)
            return carry

        lax.fori_loop(0, local_blocks, one, 0)

    def backward_units(t, a, b):
        arrive(a)

        def one(g, carry):
            units_in(a, g)
            for u in range(TILE):
                i = g * TILE + u
                held = kept[t, i]
                mixed = regrouped[u]
                pre = contract(up_turned[i], held, 1, 0)
                back_act = contract(down_turned[i], mixed, 1, 0)
                square, bent, half = gelu_parts(pre)
                act = (pre * half).astype(BF)
                slope = half + (0.5 * ROOT) * pre * (1.0 - bent * bent) * (
                    1.0 + (3.0 * CUBE) * square
                )
                back_pre = (back_act * slope).astype(BF)
                staged[u] = contract(up_small[i], back_pre, 1, 0).astype(BF)
                grad_up = contract(held, back_pre, 1, 1)
                grad_down = contract(mixed, act, 1, 1)
                if t == 0:
                    sum_up[i] = grad_up
                    sum_down[i] = grad_down
                elif t + 1 < ticks:
                    sum_up[i] += grad_up
                    sum_down[i] += grad_down
                else:
                    up_turned_out = (sum_up[i] + grad_up).astype(BF)
                    down_turned_out = (sum_down[i] + grad_down).astype(BF)
                    kept[0, i] = up_turned_out
                    kept[t, i] = down_turned_out
            units_out(b, g)
            return carry

        lax.fori_loop(0, groups, one, 0)

    def backward_out(t, b):
        arrive(b)

        def one(j, carry):
            column = pl.ds(pl.multiple_of(j * width, LANES), width)
            back_in = contract(block_of(b, j), up_big[j], 0, 1)
            made_cot[t, :, column] = (
                g_in[t, :, column].astype(F32) + back_in
            ).astype(BF)
            if t + 1 < ticks:

                @pl.when(sec > 0)
                def _():
                    shift(t + 1, j, made_cot.at[t], False).start()

            return carry

        lax.fori_loop(0, local_blocks, one, 0)

    end = ticks - 1
    stores = [
        pltpu.make_async_copy(made_out.at[end], out_ref, store_sem.at[0]),
        pltpu.make_async_copy(kept.at[0], grad_up_ref, store_sem.at[1]),
        pltpu.make_async_copy(kept.at[end], grad_down_ref, store_sem.at[2]),
        pltpu.make_async_copy(made_cot.at[end], cot_ref, store_sem.at[3]),
    ]

    def stage(kind, t):
        a = 4 * t
        if kind == "FB":
            forward_blocks(t, a)
        elif kind == "FU":
            forward_units(t, a, a + 1)
        elif kind == "FO":
            forward_out(t, a + 1)
            if t == end:
                stores[0].start()
        elif kind == "BB":
            backward_blocks(t, a + 2)
        elif kind == "BU":
            backward_units(t, a + 2, a + 3)
            if t == end:
                stores[1].start()
                stores[2].start()
        else:
            backward_out(t, a + 3)
            if t == end:
                stores[3].start()

    def only(who, *steps):
        @pl.when(who)
        def _():
            for kind, t in steps:
                stage(kind, t)

    for t in range(ticks):
        early, late = (is_even, is_odd) if t % 2 == 0 else (is_odd, is_even)
        only(early, ("BB", t))
        stage("FB", t)
        if t > 0:
            only(is_last, ("BO", t - 1))
        only(late, ("BB", t))
        only(early, ("BU", t))
        stage("FU", t)
        only(late, ("BU", t))
        only(early, ("BO", t))
        stage("FO", t)
        only(late, ("BO", t))
        only(is_last, ("BB", t), ("BU", t))
    only(is_last, ("BO", end))

    for t in range(ticks):
        for which, far in ((0, 0), (1, last)):

            @pl.when(sec != far)
            def _():
                to_end(t, which, far).wait_send()

        @pl.when(sec < last)
        def _():
            pltpu.make_async_remote_copy(
                made_out.at[0],
                x_in.at[t],
                x_send.at[t],
                x_recv.at[t, 0],
                device_id=(sec + 1, blk),
                device_id_type=MESH,
            ).wait_send()

        @pl.when(sec > 0)
        def _():
            pltpu.make_async_remote_copy(
                made_cot.at[0],
                g_in.at[t],
                g_send.at[t],
                g_recv.at[t, 0],
                device_id=(sec - 1, blk),
                device_id_type=MESH,
            ).wait_send()

    for a in range(4 * ticks):
        for k in range(1, parts):
            whole(a, k).wait_send()
    for store in stores:
        store.wait()


def local(
    held_outputs,
    held_cotangents,
    new_rows,
    targets,
    saved_first,
    up_first,
    up_second,
    down_first,
    down_second,
):
    sections = lax.axis_size("section")
    parts = lax.axis_size("blk")
    count, features = held_outputs.shape[1:]
    ticks, per = new_rows.shape[:2]
    local_blocks, width = up_first.shape[1:3]
    slab, all_blocks, hidden = up_second.shape[1:]
    exchanges = 4 * ticks

    def piece(rows):
        tiles = rows.reshape(ticks, per, features // LANES, LANES)
        return tiles.transpose(0, 2, 1, 3).reshape(ticks, per * features // LANES, LANES)

    saved = saved_first[0].transpose(0, 3, 2, 1)
    anywhere = pl.BlockSpec(memory_space=pl.ANY)
    vmem = pltpu.VMEM
    dma = pltpu.SemaphoreType.DMA
    outs = pl.pallas_call(
        functools.partial(kernel, sections, parts),
        out_shape=(
            jax.ShapeDtypeStruct((count, features), BF),
            jax.ShapeDtypeStruct((count, features), BF),
            jax.ShapeDtypeStruct((slab, all_blocks, hidden), BF),
            jax.ShapeDtypeStruct((slab, all_blocks, hidden), BF),
        ),
        in_specs=[anywhere] * 9,
        out_specs=(anywhere,) * 4,
        scratch_shapes=[
            vmem((local_blocks, width, width), BF),
            vmem((local_blocks, width, width), BF),
            vmem((slab, all_blocks, hidden), BF),
            vmem((slab, all_blocks, hidden), BF),
            vmem((slab, hidden, all_blocks), BF),
            vmem((slab, hidden, all_blocks), BF),
            vmem((ticks, slab, all_blocks, count), BF),
            vmem((ticks, count, features), BF),
            vmem((ticks, count, features), BF),
            vmem((ticks, count, features), BF),
            vmem((ticks, count, features), BF),
            vmem((exchanges, all_blocks, slab, count), BF),
            vmem((exchanges, all_blocks, slab, count), BF),
            vmem((TILE, all_blocks, count), BF),
            vmem((TILE, all_blocks, count), BF),
            vmem((slab, all_blocks, hidden), F32),
            vmem((slab, all_blocks, hidden), F32),
            vmem((ticks, sections, per * features // LANES, LANES), BF),
            vmem((ticks, count, features), BF),
            vmem((TILE * TILE, TILE * TILE), BF),
            vmem((TILE * TILE, TILE * TILE), BF),
            dma((4,)),
            dma((ticks,)),
            dma((ticks,)),
            dma((ticks, 2)),
            dma((ticks,)),
            dma((ticks,)),
            dma((ticks, local_blocks)),
            dma((ticks,)),
            dma((ticks, local_blocks)),
            dma((exchanges, parts)),
            dma((exchanges, parts)),
            dma((4,)),
        ],
        compiler_params=pltpu.CompilerParams(
            collective_id=0, has_side_effects=True, vmem_limit_bytes=60 * 1024 * 1024
        ),
        name="relay_window",
    )(
        held_outputs[0],
        held_cotangents[0],
        piece(new_rows),
        piece(targets),
        saved,
        up_first[0],
        up_second[0],
        down_first[0],
        down_second[0],
    )
    return tuple(out[None] for out in outs)


def solution(mesh):
    placed = (
        P("section", None, "blk"),
        P("section", None, "blk"),
        P(None, "section", "blk"),
        P(None, "section", "blk"),
        P("section", None, None, None, "blk"),
        P("section", "blk", None, None),
        P("section", "blk", None, None),
        P("section", "blk", None, None),
        P("section", "blk", None, None),
    )
    return jax.shard_map(
        local,
        mesh=mesh,
        in_specs=placed,
        out_specs=(
            P("section", None, "blk"),
            P("section", None, "blk"),
            P("section", "blk", None, None),
            P("section", "blk", None, None),
        ),
        check_vma=False,
    )
```
